32 devices in a mesh: region: 4 (over y, core), block: 8 (over z, x).
Axes of the slice: x: 2, y: 2, z: 4, core: 2. Of those that a mesh axis runs over, the one named last changes fastest.
Arguments:
- features: bfloat16 [24576, 128], P(('region', 'block')), may hold values from -6 to 6
- grad_out: bfloat16 [24576, 128], P(('region', 'block')), may hold values from -6 to 6
- w1: bfloat16 [27, 128, 128], replicated, may hold values from -0.109375 to 0.109375
- w2: bfloat16 [27, 128, 128], replicated, may hold values from -0.109375 to 0.109375
- rulebook: int32 [27, 24576], P(None, ('region', 'block')), may hold values from 0 to 1024, as said below
- live_blocks: int32 [192], P(('region', 'block')), may hold values from 0 to 1, as said below
Outputs:
- grad_in: bfloat16 [24576, 128], P(('region', 'block'))
- grad_w1: float32 [27, 128, 128], replicated
- grad_w2: float32 [27, 128, 128], replicated
The draws below stay inside these ranges and needn't reach their ends.
Inputs may be any that keep to these rules, and one draw needn't show every extreme that they name: `rulebook`: entries index slab s's extended rows as in the reference program; the value 768 + 2 * 128 means no neighbour. Every entry of a padded row has that value; no entry points at a padded row or at a missing neighbour; offset 27 // 2 of a live row points at the row itself. An entry of row v of slab s other than 1024 lies between v - s * 768 and v - s * 768 + 2 * 128. `live_blocks`: the first 1 and the last 1 block of every slab are live; the padded blocks of a slab lie between them. Some slab has all 6 blocks live and some slab only 2.
All inputs are finite; a program needn't handle non-finite values.
Results may differ from the reference program's by a relative error of at most 0.0039.
Values may be sent and summed in bfloat16 or wider, within the bound.
A program may use at most 64 MiB of HBM per device.

```python
import jax
import jax.numpy as jnp
from jax import lax

C = 128
K = 27
BLOCK = 128
NB = 6
HB = 1
ROWS_DEV = 768
HALO = 128
SLABS = 8
VOXELS = 24576


def slab_layout(key):
    base = jax.random.fold_in(key, 4711)
    key_count, key_shift, key_keep = jax.random.split(base, 3)
    slab_count = VOXELS // ROWS_DEV
    counts = jax.random.randint(key_count, (slab_count,), 2 * HB, NB + 1)
    counts = counts.at[0].set(NB).at[1].set(2 * HB)
    block_ids = jnp.arange(NB)
    live = (block_ids[None, :] < counts[:, None] - HB) | (block_ids[None, :] >= NB - HB)
    live = live.astype(jnp.int32)
    row_live = jnp.repeat(live, BLOCK, axis=1)
    shifts = jax.random.randint(key_shift, (K, slab_count, ROWS_DEV), -HALO, HALO + 1)
    center = (jnp.arange(K) == K // 2)[:, None, None]
    shifts = jnp.where(center, 0, shifts)
    keeper = (jax.random.randint(key_keep, (K, slab_count, ROWS_DEV), 0, 4) > 0) | center
    target = jnp.arange(ROWS_DEV)[None, None, :] + shifts
    position = (jnp.arange(slab_count) % SLABS)[None, :, None]
    inside = ((target >= 0) | (position > 0)) & ((target < ROWS_DEV) | (position < SLABS - 1))
    clipped = jnp.clip(target, 0, ROWS_DEV - 1)
    target_live = jnp.take_along_axis(jnp.broadcast_to(row_live[None], (K, slab_count, ROWS_DEV)), clipped, axis=2)
    target_live = jnp.where((target >= 0) & (target < ROWS_DEV), target_live, 1)
    usable = keeper & inside & (target_live == 1) & (row_live[None] == 1)
    rule_table = jnp.where(usable, target + HALO, ROWS_DEV + 2 * HALO).astype(jnp.int32)
    return (rule_table.reshape(K, slab_count * ROWS_DEV), live.reshape(slab_count * NB))


def draw_rulebook(key, part):
    return slab_layout(key)[0]


def draw_live_blocks(key, part):
    return slab_layout(key)[1]


def level_of(key, dims, cuts, least, largest):
    def one(dim, parts):
        heights = jax.random.uniform(jax.random.fold_in(jax.random.fold_in(key, 6), dim), (parts,), jnp.float32, least / len(cuts), largest / len(cuts))
        return jnp.repeat(jnp.exp(heights), dims[dim] // parts).reshape((-1,) + (1,) * (len(dims) - dim - 1))

    factor_of = one(*cuts[0])
    for cut in cuts[1:]:
        factor_of = factor_of * one(*cut)
    return factor_of


def scatter_about(stream_key, dims, deviation, reach, cuts=(), held_as=jnp.bfloat16):
    drawn = deviation * jax.random.normal(stream_key, dims, jnp.float32)
    if cuts:
        drawn = drawn * level_of(stream_key, dims, cuts, -0.22, 0.18)
    return jnp.clip(drawn, -reach, reach).astype(held_as)


def setup_inputs(seed: int = 0) -> dict:
    key_of = jax.random.split(jax.random.key(seed), 7)
    return {
        "features": scatter_about(key_of[0], (VOXELS, C), 1.0, 6.0, ((0, 32),)),
        "grad_out": scatter_about(key_of[1], (VOXELS, C), 1.0, 6.0, ((0, 32),)),
        "w1": scatter_about(key_of[2], (K, C, C), (K * C) ** -0.5, 0.109375),
        "w2": scatter_about(key_of[3], (K, C, C), (K * C) ** -0.5, 0.109375),
        "rulebook": draw_rulebook(jax.random.fold_in(key_of[6], 71), 0),
        "live_blocks": draw_live_blocks(jax.random.fold_in(key_of[6], 71), 0),
    }


def dsilu(hidden):
    sigma = jax.nn.sigmoid(hidden)
    return sigma * (1.0 + hidden * (1.0 - sigma))

def extend(values):
    slab_count = values.shape[0]
    chans = values.shape[2]
    position = jnp.arange(slab_count) % SLABS
    rim_zeros = jnp.zeros((1, HALO, chans), values.dtype)
    before = jnp.concatenate([rim_zeros, values[:-1, ROWS_DEV - HALO:]], 0)
    before = jnp.where((position > 0)[:, None, None], before, jnp.zeros_like(before))
    after = jnp.concatenate([values[1:, :HALO], rim_zeros], 0)
    after = jnp.where((position < SLABS - 1)[:, None, None], after, jnp.zeros_like(after))
    blank = jnp.zeros((slab_count, 1, chans), values.dtype)
    return jnp.concatenate([before, values, after, blank], 1)

def gather_rows(extended, lookup):
    return jax.vmap(lambda source, picks: source[picks])(extended, lookup)

def fold_back(scattered):
    slab_count = scattered.shape[0]
    chans = scattered.shape[2]
    position = jnp.arange(slab_count) % SLABS
    own_rows = scattered[:, HALO:HALO + ROWS_DEV]
    lower_rim = scattered[:, :HALO]
    upper_rim = scattered[:, HALO + ROWS_DEV:2 * HALO + ROWS_DEV]
    rim_zeros = jnp.zeros((1, HALO, chans), scattered.dtype)
    from_above = jnp.concatenate([lower_rim[1:], rim_zeros], 0)
    from_above = jnp.where((position < SLABS - 1)[:, None, None], from_above, jnp.zeros_like(from_above))
    from_below = jnp.concatenate([rim_zeros, upper_rim[:-1]], 0)
    from_below = jnp.where((position > 0)[:, None, None], from_below, jnp.zeros_like(from_below))
    own_rows = own_rows.at[:, :HALO].add(from_below)
    own_rows = own_rows.at[:, ROWS_DEV - HALO:].add(from_above)
    return own_rows

def reference(features, grad_out, w1, w2, rulebook, live_blocks):
    slab_count = VOXELS // ROWS_DEV
    rule_table = rulebook.reshape(K, slab_count, ROWS_DEV)
    ext_feat = extend(features.reshape(slab_count, ROWS_DEV, C))

    def forward(running, pair):
        weight, lookup = pair
        picked = gather_rows(ext_feat, lookup).reshape(-1, C)
        return (running + jnp.dot(picked, weight, preferred_element_type=jnp.float32), None)
    hidden, _ = lax.scan(forward, jnp.zeros((VOXELS, C), jnp.float32), (w1, rule_table))
    act = jax.nn.silu(hidden).astype(jnp.bfloat16)
    ext_act = extend(act.reshape(slab_count, ROWS_DEV, C))
    scale = jnp.sqrt(jnp.float32(VOXELS))

    def kernel_grad(extended, right_side):

        def step(running, lookup):
            picked = gather_rows(extended, lookup).reshape(-1, C)
            return (running, jnp.dot(picked.T, right_side, preferred_element_type=jnp.float32))
        _, grads = lax.scan(step, jnp.zeros((), jnp.float32), rule_table)
        return grads / scale

    def scatter_back(source, weights):
        start = jnp.zeros((slab_count, ROWS_DEV + 2 * HALO + 1, C), jnp.float32)

        def step(running, pair):
            weight, lookup = pair
            spread = jnp.dot(source, weight.T, preferred_element_type=jnp.float32).reshape(slab_count, ROWS_DEV, C)
            added = jax.vmap(lambda target, picks, terms: target.at[picks].add(terms))(running, lookup, spread)
            return (added, None)
        scattered, _ = lax.scan(step, start, (weights, rule_table))
        return fold_back(scattered).reshape(VOXELS, C)
    grad_w2 = kernel_grad(ext_act, grad_out)
    grad_act = scatter_back(grad_out, w2)
    grad_hidden = (grad_act * dsilu(hidden)).astype(jnp.bfloat16)
    grad_w1 = kernel_grad(ext_feat, grad_hidden)
    grad_feat = scatter_back(grad_hidden, w1)
    live = jnp.repeat(live_blocks, BLOCK).astype(jnp.float32)[:, None]
    grad_in = (live * (grad_out.astype(jnp.float32) + grad_feat)).astype(jnp.bfloat16)
    return (grad_in, grad_w1, grad_w2)
```

```python
import functools

import jax
import jax.numpy as jnp
from jax import lax
from jax.experimental import pallas as pl
from jax.experimental.pallas import tpu as pltpu
from jax.sharding import PartitionSpec as P

BLOCK = 128
HALO = 128
PAD = 2 * HALO
MESH = pl.DeviceIdType.MESH
F32 = jnp.float32
BF16 = jnp.bfloat16


def one_hot(matches):
    return jnp.where(matches, 1.0, 0.0).astype(BF16)


def groups_of(count):
    return 9 if count % 9 == 0 else 1


def slab_kernel(
    length,
    feat, gout, w1, w2, rule, rule_t, live,
    grad_in, partial,
    fext, aext, gpad, hpad, rpad, wc, hots, spread, spread2, picks, hidden, gext, rims, rim_in,
    send, recv,
):
    rows, chans = feat.shape
    offsets = w1.shape[0]
    blocks = rows // BLOCK
    ext_blocks = blocks + 2
    window = 3 * BLOCK
    group = groups_of(offsets)
    part_rows = partial.shape[1]
    me = lax.axis_index("block")
    left, right = me - 1, me + 1
    has_left, has_right = me > 0, me < length - 1

    def copies(i, low, low_there, high, high_there):
        down = pltpu.make_async_remote_copy(
            src_ref=low, dst_ref=low_there, send_sem=send.at[i, 0], recv_sem=recv.at[i, 0],
            device_id={"block": left}, device_id_type=MESH)
        up = pltpu.make_async_remote_copy(
            src_ref=high, dst_ref=high_there, send_sem=send.at[i, 1], recv_sem=recv.at[i, 1],
            device_id={"block": right}, device_id_type=MESH)
        return down, up

    def start(pair):
        down, up = pair
        pl.when(has_left)(down.start)
        pl.when(has_right)(up.start)

    def finish(pair):
        down, up = pair

        @pl.when(has_left)
        def _():
            down.wait_send()
            up.wait_recv()

        @pl.when(has_right)
        def _():
            up.wait_send()
            down.wait_recv()

    barrier = pltpu.get_barrier_semaphore()

    @pl.when(has_left)
    def _():
        pl.semaphore_signal(barrier, inc=1, device_id={"block": left}, device_id_type=MESH)

    @pl.when(has_right)
    def _():
        pl.semaphore_signal(barrier, inc=1, device_id={"block": right}, device_id_type=MESH)

    pl.semaphore_wait(barrier, has_left.astype(jnp.int32) + has_right.astype(jnp.int32))

    lower, upper = pl.ds(0, HALO), pl.ds(HALO + rows, HALO)
    own_low, own_high = pl.ds(HALO, HALO), pl.ds(rows, HALO)
    feat_copies = copies(0, feat.at[pl.ds(0, HALO)], fext.at[upper],
                         feat.at[pl.ds(rows - HALO, HALO)], fext.at[lower])
    act_copies = copies(1, aext.at[own_low], aext.at[upper], aext.at[own_high], aext.at[lower])
    rim_copies = [
        copies(2 + i, rims.at[i, 0], rim_in.at[i, 0], rims.at[i, 1], rim_in.at[i, 1])
        for i in range(2)
    ]
    start(feat_copies)

    edge = jnp.zeros((HALO, chans), BF16)

    @pl.when(jnp.logical_not(has_left))
    def _():
        fext[lower] = edge
        aext[lower] = edge
        for i in range(2):
            rim_in[i, 1] = edge

    @pl.when(jnp.logical_not(has_right))
    def _():
        fext[upper] = edge
        aext[upper] = edge
        for i in range(2):
            rim_in[i, 0] = edge

    fext[pl.ds(HALO, rows)] = feat[...]
    border = jnp.zeros((PAD, chans), BF16)
    for padded in (gpad, hpad):
        padded[pl.ds(0, PAD)] = border
        padded[pl.ds(PAD + rows, PAD)] = border
    gpad[pl.ds(PAD, rows)] = gout[...]
    nowhere = jnp.full((offsets, PAD), -1, jnp.int32)
    rpad[:, pl.ds(0, PAD)] = nowhere
    rpad[:, pl.ds(PAD + rows, PAD)] = nowhere
    rpad[:, pl.ds(PAD, rows)] = rule[...]

    def beside(weights):
        for k in range(offsets):
            wc[:, k * chans:(k + 1) * chans] = weights[k]

    def spread_rows(e, first, out, source):
        begin = pl.multiple_of(e * BLOCK, BLOCK)
        got = jnp.dot(hots[e, first * BLOCK:(first + group) * BLOCK, :],
                      source[pl.ds(begin, window)], preferred_element_type=F32).astype(BF16)
        for j in range(group):
            out[pl.ds(begin, BLOCK), (first + j) * chans:(first + j + 1) * chans] = (
                got[j * BLOCK:(j + 1) * BLOCK])

    def through_weights(source, i):
        @pl.loop(0, ext_blocks)
        def _(e):
            begin = pl.multiple_of(e * BLOCK, BLOCK)
            gext[pl.ds(begin, BLOCK)] = lax.dot_general(
                source[pl.ds(begin, BLOCK)], wc[...], (((1,), (1,)), ((), ())),
                preferred_element_type=F32)
        rims[i, 0] = gext[lower].astype(BF16)
        rims[i, 1] = gext[upper].astype(BF16)
        start(rim_copies[i])

    def take_rims(i):
        finish(rim_copies[i])
        gext[own_low] = gext[own_low] + rim_in[i, 1].astype(F32)
        gext[own_high] = gext[own_high] + rim_in[i, 0].astype(F32)

    def kernel_grad(extended, source, i):
        turned = extended[...].T

        @pl.loop(0, offsets // 3)
        def _(g):
            begin = pl.multiple_of(g * 3 * chans, chans)
            got = jnp.dot(turned, source[:, pl.ds(begin, 3 * chans)], preferred_element_type=F32)
            for j in range(3):
                at = pl.multiple_of((g * 3 + j) * chans, chans)
                partial[i, pl.ds(at, chans)] = got[:, j * chans:(j + 1) * chans]
        tail = part_rows - offsets * chans
        if tail:
            partial[i, pl.ds(offsets * chans, tail)] = jnp.zeros((tail, chans), F32)

    @pl.loop(0, ext_blocks)
    def _(e):
        begin = pl.multiple_of(e * BLOCK, BLOCK)
        target = lax.broadcasted_iota(jnp.int32, (BLOCK, window), 0) + e * BLOCK
        for first in range(0, offsets, group):
            for k in range(first, first + group):
                hots[e, k * BLOCK:(k + 1) * BLOCK, :] = one_hot(
                    rpad[k:k + 1, pl.ds(begin, window)] == target)
            spread_rows(e, first, spread, gpad)

    beside(w2)
    through_weights(spread, 0)

    finish(feat_copies)

    @pl.loop(0, blocks)
    def _(b):
        begin = pl.multiple_of(b * BLOCK, BLOCK)
        local = rule_t[pl.ds(begin, BLOCK)] - b * BLOCK
        columns = lax.broadcasted_iota(jnp.int32, (BLOCK, window), 1)
        framed = fext[pl.ds(begin, window)]
        for first in range(0, offsets, group):
            chosen = jnp.concatenate(
                [one_hot(local[:, k:k + 1] == columns) for k in range(first, first + group)], 0)
            got = jnp.dot(chosen, framed, preferred_element_type=F32).astype(BF16)
            for j in range(group):
                picks[:, (first + j) * chans:(first + j + 1) * chans] = (
                    got[j * BLOCK:(j + 1) * BLOCK])
        total = jnp.dot(picks[...], w1[...].reshape(offsets * chans, chans),
                        preferred_element_type=F32)
        hidden[pl.ds(begin, BLOCK)] = total
        aext[pl.ds(begin + HALO, BLOCK)] = (total / (1.0 + jnp.exp(-total))).astype(BF16)

    start(act_copies)
    take_rims(0)

    @pl.loop(0, blocks)
    def _(b):
        begin = pl.multiple_of(b * BLOCK, BLOCK)
        value = hidden[pl.ds(begin, BLOCK)]
        sigma = 1.0 / (1.0 + jnp.exp(-value))
        slope = sigma * (1.0 + value * (1.0 - sigma))
        hpad[pl.ds(begin + PAD, BLOCK)] = (gext[pl.ds(begin + HALO, BLOCK)] * slope).astype(BF16)

    @pl.loop(0, ext_blocks)
    def _(e):
        for first in range(0, offsets, group):
            spread_rows(e, first, spread2, hpad)

    beside(w1)
    through_weights(spread2, 1)
    kernel_grad(fext, spread2, 0)
    finish(act_copies)
    kernel_grad(aext, spread, 1)
    take_rims(1)
    for b in range(blocks):
        at = pl.ds(b * BLOCK, BLOCK)
        keep = live[b].astype(F32)
        grad_in[at] = (keep * (gout[at].astype(F32) + gext[pl.ds(b * BLOCK + HALO, BLOCK)])
                       ).astype(BF16)


def slab_step(features, grad_out, w1, w2, rulebook, live_blocks, part_rows):
    rows, chans = features.shape
    offsets = w1.shape[0]
    ext = rows + 2 * HALO
    blocks = rows // BLOCK
    wide = offsets * chans
    vmem = pl.BlockSpec(memory_space=pltpu.VMEM)
    return pl.pallas_call(
        functools.partial(slab_kernel, lax.axis_size("block")),
        out_shape=(
            jax.ShapeDtypeStruct((rows, chans), BF16),
            jax.ShapeDtypeStruct((2, part_rows, chans), F32),
        ),
        in_specs=[vmem] * 6 + [pl.BlockSpec(memory_space=pltpu.SMEM)],
        out_specs=(vmem, vmem),
        scratch_shapes=[
            pltpu.VMEM((ext, chans), BF16),
            pltpu.VMEM((ext, chans), BF16),
            pltpu.VMEM((rows + 2 * PAD, chans), BF16),
            pltpu.VMEM((rows + 2 * PAD, chans), BF16),
            pltpu.VMEM((offsets, rows + 2 * PAD), jnp.int32),
            pltpu.VMEM((chans, wide), BF16),
            pltpu.VMEM((blocks + 2, offsets * BLOCK, 3 * BLOCK), BF16),
            pltpu.VMEM((ext, wide), BF16),
            pltpu.VMEM((ext, wide), BF16),
            pltpu.VMEM((BLOCK, wide), BF16),
            pltpu.VMEM((rows, chans), F32),
            pltpu.VMEM((ext, chans), F32),
            pltpu.VMEM((2, 2, HALO, chans), BF16),
            pltpu.VMEM((2, 2, HALO, chans), BF16),
            pltpu.SemaphoreType.DMA((4, 2)),
            pltpu.SemaphoreType.DMA((4, 2)),
        ],
        compiler_params=pltpu.CompilerParams(
            collective_id=0, has_side_effects=True, vmem_limit_bytes=64000000),
    )(features, grad_out, w1, w2, rulebook, rulebook.T, live_blocks)


def sum_kernel(region, block, scale, part, out, own, mine, rest, got1, got2, got3,
               send, recv, send_back, recv_back):
    total = part.shape[0]
    planes, depth = region // 2 * 2, block // 2
    half = total // 2
    quarter = half // planes
    piece = quarter // depth
    r, b = lax.axis_index("region"), lax.axis_index("block")
    c, y, x, z = lax.rem(r, 2), r // 2, lax.rem(b, 2), b // 2
    p = y * 2 + x

    def device(core, plane, deep):
        return {"region": plane // 2 * 2 + core, "block": deep * 2 + lax.rem(plane, 2)}

    partner = device(1 - c, p, z)
    plane_peers = [device(c, lax.rem(p + d, planes), z) for d in range(1, planes)]
    deep_peers = [device(c, p, lax.rem(z + d, depth)) for d in range(1, depth)]
    barrier = pltpu.get_barrier_semaphore()
    for peer in [partner] + plane_peers + deep_peers:
        pl.semaphore_signal(barrier, inc=1, device_id=peer, device_id_type=MESH)
    pl.semaphore_wait(barrier, planes + depth - 1)

    def at(index, size):
        return pl.ds(pl.multiple_of(index * size, 16), size)

    def remote(src, dst, sems, i, peer):
        return pltpu.make_async_remote_copy(
            src_ref=src, dst_ref=dst, send_sem=sems[0].at[i], recv_sem=sems[1].at[i],
            device_id=peer, device_id_type=MESH)

    there = (send, recv)
    back = (send_back, recv_back)
    first = remote(part.at[at(1 - c, half)], got1, there, 0, partner)
    first.start()
    first.wait()
    mine[...] = (part[at(c, half)] + got1[...]).astype(BF16)
    second = []
    for d in range(1, planes):
        second.append(remote(mine.at[at(lax.rem(p + d, planes), quarter)], got2.at[d - 1],
                             there, d, plane_peers[d - 1]))
        second[-1].start()
    value = part[at(c * planes + p, quarter)] + got1[at(p, quarter)]
    for d in range(1, planes):
        second[d - 1].wait()
        value = value + got2[d - 1].astype(F32)
    own[...] = value
    rest[...] = value.astype(BF16)
    third = []
    for d in range(1, depth):
        third.append(remote(rest.at[at(lax.rem(z + d, depth), piece)], got3.at[d - 1],
                            there, planes - 1 + d, deep_peers[d - 1]))
        third[-1].start()
    value = own[at(z, piece)]
    for d in range(1, depth):
        third[d - 1].wait()
        value = value + got3[d - 1].astype(F32)
    place = at((c * planes + p) * depth + z, piece)
    out[place] = (value / scale).astype(BF16)
    for where, peers, base in (
        (place, deep_peers, planes),
        (at(c * planes + p, quarter), plane_peers, 1),
        (at(c, half), [partner], 0),
    ):
        moved = [remote(out.at[where], out.at[where], back, base + i, peer)
                 for i, peer in enumerate(peers)]
        for copy in moved:
            copy.start()
        for copy in moved:
            copy.wait()


def summed(part, scale):
    region, block = lax.axis_size("region"), lax.axis_size("block")
    total, chans = part.shape
    planes, depth = region // 2 * 2, block // 2
    half = total // 2
    quarter = half // planes
    piece = quarter // depth
    count = planes + depth - 1
    vmem = pl.BlockSpec(memory_space=pltpu.VMEM)
    return pl.pallas_call(
        functools.partial(sum_kernel, region, block, scale),
        out_shape=jax.ShapeDtypeStruct((total, chans), BF16),
        in_specs=[vmem],
        out_specs=vmem,
        scratch_shapes=[
            pltpu.VMEM((quarter, chans), F32),
            pltpu.VMEM((half, chans), BF16),
            pltpu.VMEM((quarter, chans), BF16),
            pltpu.VMEM((half, chans), F32),
            pltpu.VMEM((planes - 1, quarter, chans), BF16),
            pltpu.VMEM((depth - 1, piece, chans), BF16),
        ] + [pltpu.SemaphoreType.DMA((count,))] * 4,
        compiler_params=pltpu.CompilerParams(collective_id=1, has_side_effects=True),
    )(part)


def on_device(features, grad_out, w1, w2, rulebook, live_blocks):
    offsets, chans = w1.shape[0], w1.shape[1]
    devices = lax.axis_size("region") * lax.axis_size("block")
    step = 16 * devices
    part_rows = (offsets * chans + step - 1) // step * step
    grad_in, partial = slab_step(
        features, grad_out, w1, w2, rulebook, live_blocks, part_rows)
    scale = float(features.shape[0] * devices) ** 0.5
    both = summed(partial.reshape(2 * part_rows, chans), scale)
    both = both.reshape(2, part_rows, chans)[:, :offsets * chans].astype(F32)
    both = both.reshape(2, offsets, chans, chans)
    return (grad_in, both[0], both[1])


def solution(mesh):
    return jax.shard_map(
        on_device,
        mesh=mesh,
        in_specs=(
            P(("region", "block"), None),
            P(("region", "block"), None),
            P(),
            P(),
            P(None, ("region", "block")),
            P(("region", "block")),
        ),
        out_specs=(P(("region", "block"), None), P(), P()),
        check_vma=False,
    )
```

```python
import functools

import jax
import jax.numpy as jnp
from jax import lax
from jax.experimental import pallas as pl
from jax.experimental.pallas import tpu as pltpu
from jax.sharding import PartitionSpec as P

BLOCK = 128
HALO = 128
PAD = 2 * HALO
MESH = pl.DeviceIdType.MESH
F32 = jnp.float32
BF16 = jnp.bfloat16


def one_hot(matches):
    return jnp.where(matches, 1.0, 0.0).astype(BF16)


def groups_of(count):
    return 9 if count % 9 == 0 else 1


def slab_kernel(
    region, length, scale,
    feat, gout, w1, w2, rule, rule_t, live,
    grad_in, total_out,
    fext, aext, gpad, hpad, rpad, wc, hots, spread, spread2, picks, hidden, gext, rims, rim_in,
    send, recv, partial, own, mine, rest, got1, got2, got3,
    send_there, recv_there, send_back, recv_back,
):
    rows, chans = feat.shape
    offsets = w1.shape[0]
    blocks = rows // BLOCK
    ext_blocks = blocks + 2
    window = 3 * BLOCK
    group = groups_of(offsets)
    part_rows = partial.shape[1]
    me = lax.axis_index("block")
    left, right = me - 1, me + 1
    has_left, has_right = me > 0, me < length - 1

    def copies(i, low, low_there, high, high_there):
        down = pltpu.make_async_remote_copy(
            src_ref=low, dst_ref=low_there, send_sem=send.at[i, 0], recv_sem=recv.at[i, 0],
            device_id={"block": left}, device_id_type=MESH)
        up = pltpu.make_async_remote_copy(
            src_ref=high, dst_ref=high_there, send_sem=send.at[i, 1], recv_sem=recv.at[i, 1],
            device_id={"block": right}, device_id_type=MESH)
        return down, up

    def start(pair):
        down, up = pair
        pl.when(has_left)(down.start)
        pl.when(has_right)(up.start)

    def finish(pair):
        down, up = pair

        @pl.when(has_left)
        def _():
            down.wait_send()
            up.wait_recv()

        @pl.when(has_right)
        def _():
            up.wait_send()
            down.wait_recv()

    stages, peers = sum_stages(
        region, length, scale, partial, total_out, own, mine, rest, got1, got2, got3,
        send_there, recv_there, send_back, recv_back)
    barrier = pltpu.get_barrier_semaphore()
    for peer in peers:
        pl.semaphore_signal(barrier, inc=1, device_id=peer, device_id_type=MESH)

    @pl.when(has_left)
    def _():
        pl.semaphore_signal(barrier, inc=1, device_id={"block": left}, device_id_type=MESH)

    @pl.when(has_right)
    def _():
        pl.semaphore_signal(barrier, inc=1, device_id={"block": right}, device_id_type=MESH)

    pl.semaphore_wait(
        barrier, len(peers) + has_left.astype(jnp.int32) + has_right.astype(jnp.int32))

    lower, upper = pl.ds(0, HALO), pl.ds(HALO + rows, HALO)
    own_low, own_high = pl.ds(HALO, HALO), pl.ds(rows, HALO)
    feat_copies = copies(0, feat.at[pl.ds(0, HALO)], fext.at[upper],
                         feat.at[pl.ds(rows - HALO, HALO)], fext.at[lower])
    act_copies = copies(1, aext.at[own_low], aext.at[upper], aext.at[own_high], aext.at[lower])
    rim_copies = [
        copies(2 + i, rims.at[i, 0], rim_in.at[i, 0], rims.at[i, 1], rim_in.at[i, 1])
        for i in range(2)
    ]
    start(feat_copies)

    edge = jnp.zeros((HALO, chans), BF16)

    @pl.when(jnp.logical_not(has_left))
    def _():
        fext[lower] = edge
        aext[lower] = edge
        for i in range(2):
            rim_in[i, 1] = edge

    @pl.when(jnp.logical_not(has_right))
    def _():
        fext[upper] = edge
        aext[upper] = edge
        for i in range(2):
            rim_in[i, 0] = edge

    fext[pl.ds(HALO, rows)] = feat[...]
    border = jnp.zeros((PAD, chans), BF16)
    for padded in (gpad, hpad):
        padded[pl.ds(0, PAD)] = border
        padded[pl.ds(PAD + rows, PAD)] = border
    gpad[pl.ds(PAD, rows)] = gout[...]
    nowhere = jnp.full((offsets, PAD), -1, jnp.int32)
    rpad[:, pl.ds(0, PAD)] = nowhere
    rpad[:, pl.ds(PAD + rows, PAD)] = nowhere
    rpad[:, pl.ds(PAD, rows)] = rule[...]

    def beside(weights):
        for k in range(offsets):
            wc[:, k * chans:(k + 1) * chans] = weights[k]

    def spread_rows(e, first, out, source):
        begin = pl.multiple_of(e * BLOCK, BLOCK)
        got = jnp.dot(hots[e, first * BLOCK:(first + group) * BLOCK, :],
                      source[pl.ds(begin, window)], preferred_element_type=F32).astype(BF16)
        for j in range(group):
            out[pl.ds(begin, BLOCK), (first + j) * chans:(first + j + 1) * chans] = (
                got[j * BLOCK:(j + 1) * BLOCK])

    def through_weights(source, i):
        @pl.loop(0, ext_blocks)
        def _(e):
            begin = pl.multiple_of(e * BLOCK, BLOCK)
            gext[pl.ds(begin, BLOCK)] = lax.dot_general(
                source[pl.ds(begin, BLOCK)], wc[...], (((1,), (1,)), ((), ())),
                preferred_element_type=F32)
        rims[i, 0] = gext[lower].astype(BF16)
        rims[i, 1] = gext[upper].astype(BF16)
        start(rim_copies[i])

    def take_rims(i):
        finish(rim_copies[i])
        gext[own_low] = gext[own_low] + rim_in[i, 1].astype(F32)
        gext[own_high] = gext[own_high] + rim_in[i, 0].astype(F32)

    def kernel_grad(extended, source, i):
        turned = extended[...].T

        @pl.loop(0, offsets // 3)
        def _(g):
            begin = pl.multiple_of(g * 3 * chans, chans)
            got = jnp.dot(turned, source[:, pl.ds(begin, 3 * chans)], preferred_element_type=F32)
            for j in range(3):
                at = pl.multiple_of((g * 3 + j) * chans, chans)
                partial[i, pl.ds(at, chans)] = got[:, j * chans:(j + 1) * chans]
        tail = part_rows - offsets * chans
        if tail:
            partial[i, pl.ds(offsets * chans, tail)] = jnp.zeros((tail, chans), F32)

    @pl.loop(0, ext_blocks)
    def _(e):
        begin = pl.multiple_of(e * BLOCK, BLOCK)
        target = lax.broadcasted_iota(jnp.int32, (BLOCK, window), 0) + e * BLOCK
        for first in range(0, offsets, group):
            for k in range(first, first + group):
                hots[e, k * BLOCK:(k + 1) * BLOCK, :] = one_hot(
                    rpad[k:k + 1, pl.ds(begin, window)] == target)
            spread_rows(e, first, spread, gpad)

    beside(w2)
    through_weights(spread, 0)

    finish(feat_copies)

    @pl.loop(0, blocks)
    def _(b):
        begin = pl.multiple_of(b * BLOCK, BLOCK)
        local = rule_t[pl.ds(begin, BLOCK)] - b * BLOCK
        columns = lax.broadcasted_iota(jnp.int32, (BLOCK, window), 1)
        framed = fext[pl.ds(begin, window)]
        for first in range(0, offsets, group):
            chosen = jnp.concatenate(
                [one_hot(local[:, k:k + 1] == columns) for k in range(first, first + group)], 0)
            got = jnp.dot(chosen, framed, preferred_element_type=F32).astype(BF16)
            for j in range(group):
                picks[:, (first + j) * chans:(first + j + 1) * chans] = (
                    got[j * BLOCK:(j + 1) * BLOCK])
        total = jnp.dot(picks[...], w1[...].reshape(offsets * chans, chans),
                        preferred_element_type=F32)
        hidden[pl.ds(begin, BLOCK)] = total
        aext[pl.ds(begin + HALO, BLOCK)] = (total / (1.0 + jnp.exp(-total))).astype(BF16)

    start(act_copies)
    take_rims(0)

    @pl.loop(0, blocks)
    def _(b):
        begin = pl.multiple_of(b * BLOCK, BLOCK)
        value = hidden[pl.ds(begin, BLOCK)]
        sigma = 1.0 / (1.0 + jnp.exp(-value))
        slope = sigma * (1.0 + value * (1.0 - sigma))
        hpad[pl.ds(begin + PAD, BLOCK)] = (gext[pl.ds(begin + HALO, BLOCK)] * slope).astype(BF16)

    finish(act_copies)
    kernel_grad(aext, spread, 1)
    ready, later = stages(1), stages(0)
    next(ready)

    @pl.loop(0, ext_blocks)
    def _(e):
        for first in range(0, offsets, group):
            spread_rows(e, first, spread2, hpad)

    next(ready)
    kernel_grad(fext, spread2, 0)
    next(later)
    beside(w1)
    through_weights(spread2, 1)
    next(ready)
    next(later)
    take_rims(1)
    for b in range(blocks):
        at = pl.ds(b * BLOCK, BLOCK)
        keep = live[b].astype(F32)
        grad_in[at] = (keep * (gout[at].astype(F32) + gext[pl.ds(b * BLOCK + HALO, BLOCK)])
                       ).astype(BF16)
    for _ in range(4):
        next(ready)
        next(later)
    next(later, None)


def slab_step(features, grad_out, w1, w2, rulebook, live_blocks, part_rows, scale):
    region, block = lax.axis_size("region"), lax.axis_size("block")
    planes, depth = region // 2 * 2, block // 2
    half = part_rows // 2
    quarter = half // planes
    piece = quarter // depth
    count = planes + depth - 1
    rows, chans = features.shape
    offsets = w1.shape[0]
    ext = rows + 2 * HALO
    blocks = rows // BLOCK
    wide = offsets * chans
    vmem = pl.BlockSpec(memory_space=pltpu.VMEM)
    return pl.pallas_call(
        functools.partial(slab_kernel, region, block, scale),
        out_shape=(
            jax.ShapeDtypeStruct((rows, chans), BF16),
            jax.ShapeDtypeStruct((2, part_rows, chans), BF16),
        ),
        in_specs=[vmem] * 6 + [pl.BlockSpec(memory_space=pltpu.SMEM)],
        out_specs=(vmem, vmem),
        scratch_shapes=[
            pltpu.VMEM((ext, chans), BF16),
            pltpu.VMEM((ext, chans), BF16),
            pltpu.VMEM((rows + 2 * PAD, chans), BF16),
            pltpu.VMEM((rows + 2 * PAD, chans), BF16),
            pltpu.VMEM((offsets, rows + 2 * PAD), jnp.int32),
            pltpu.VMEM((chans, wide), BF16),
            pltpu.VMEM((blocks + 2, offsets * BLOCK, 3 * BLOCK), BF16),
            pltpu.VMEM((ext, wide), BF16),
            pltpu.VMEM((ext, wide), BF16),
            pltpu.VMEM((BLOCK, wide), BF16),
            pltpu.VMEM((rows, chans), F32),
            pltpu.VMEM((ext, chans), F32),
            pltpu.VMEM((2, 2, HALO, chans), BF16),
            pltpu.VMEM((2, 2, HALO, chans), BF16),
            pltpu.SemaphoreType.DMA((4, 2)),
            pltpu.SemaphoreType.DMA((4, 2)),
            pltpu.VMEM((2, part_rows, chans), F32),
            pltpu.VMEM((2, quarter, chans), F32),
            pltpu.VMEM((2, half, chans), BF16),
            pltpu.VMEM((2, quarter, chans), BF16),
            pltpu.VMEM((2, half, chans), F32),
            pltpu.VMEM((2, planes - 1, quarter, chans), BF16),
            pltpu.VMEM((2, depth - 1, piece, chans), BF16),
        ] + [pltpu.SemaphoreType.DMA((2, count))] * 4,
        compiler_params=pltpu.CompilerParams(
            collective_id=0, has_side_effects=True, vmem_limit_bytes=64000000),
    )(features, grad_out, w1, w2, rulebook, rulebook.T, live_blocks)


def sum_stages(region, block, scale, part, out, own, mine, rest, got1, got2, got3,
               send_there, recv_there, send_back, recv_back):
    half = part.shape[1] // 2
    planes, depth = region // 2 * 2, block // 2
    quarter = half // planes
    piece = quarter // depth
    r, b = lax.axis_index("region"), lax.axis_index("block")
    c, y, x, z = lax.rem(r, 2), r // 2, lax.rem(b, 2), b // 2
    p = y * 2 + x

    def device(core, plane, deep):
        return {"region": plane // 2 * 2 + core, "block": deep * 2 + lax.rem(plane, 2)}

    partner = device(1 - c, p, z)
    plane_peers = [device(c, lax.rem(p + d, planes), z) for d in range(1, planes)]
    deep_peers = [device(c, p, lax.rem(z + d, depth)) for d in range(1, depth)]

    def at(index, size):
        return pl.ds(pl.multiple_of(index * size, 16), size)

    def remote(src, dst, sems, i, n, peer):
        copy = pltpu.make_async_remote_copy(
            src_ref=src, dst_ref=dst, send_sem=sems[0].at[i, n], recv_sem=sems[1].at[i, n],
            device_id=peer, device_id_type=MESH)
        copy.start()
        return copy

    there = (send_there, recv_there)
    back = (send_back, recv_back)

    def stages(i):
        first = remote(part.at[i, at(1 - c, half)], got1.at[i], there, i, 0, partner)
        yield
        first.wait()
        mine[i] = (part[i, at(c, half)] + got1[i]).astype(BF16)
        second = [remote(mine.at[i, at(lax.rem(p + d, planes), quarter)], got2.at[i, d - 1],
                         there, i, d, plane_peers[d - 1]) for d in range(1, planes)]
        yield
        value = part[i, at(c * planes + p, quarter)] + got1[i, at(p, quarter)]
        for d in range(1, planes):
            second[d - 1].wait()
            value = value + got2[i, d - 1].astype(F32)
        own[i] = value
        rest[i] = value.astype(BF16)
        third = [remote(rest.at[i, at(lax.rem(z + d, depth), piece)], got3.at[i, d - 1],
                        there, i, planes - 1 + d, deep_peers[d - 1]) for d in range(1, depth)]
        yield
        value = own[i, at(z, piece)]
        for d in range(1, depth):
            third[d - 1].wait()
            value = value + got3[i, d - 1].astype(F32)
        place = at((c * planes + p) * depth + z, piece)
        out[i, place] = (value / scale).astype(BF16)
        for where, peers, base in (
            (place, deep_peers, planes),
            (at(c * planes + p, quarter), plane_peers, 1),
            (at(c, half), [partner], 0),
        ):
            moved = [remote(out.at[i, where], out.at[i, where], back, i, base + n, peer)
                     for n, peer in enumerate(peers)]
            yield
            for copy in moved:
                copy.wait()
        yield

    return stages, [partner] + plane_peers + deep_peers


def on_device(features, grad_out, w1, w2, rulebook, live_blocks):
    offsets, chans = w1.shape[0], w1.shape[1]
    devices = lax.axis_size("region") * lax.axis_size("block")
    step = 16 * devices
    part_rows = (offsets * chans + step - 1) // step * step
    scale = float(features.shape[0] * devices) ** 0.5
    grad_in, both = slab_step(
        features, grad_out, w1, w2, rulebook, live_blocks, part_rows, scale)
    both = both[:, :offsets * chans].astype(F32)
    both = both.reshape(2, offsets, chans, chans)
    return (grad_in, both[0], both[1])


def solution(mesh):
    return jax.shard_map(
        on_device,
        mesh=mesh,
        in_specs=(
            P(("region", "block"), None),
            P(("region", "block"), None),
            P(),
            P(),
            P(None, ("region", "block")),
            P(("region", "block")),
        ),
        out_specs=(P(("region", "block"), None), P(), P()),
        check_vma=False,
    )
```

```python
import functools

import jax
import jax.numpy as jnp
from jax import lax
from jax.experimental import pallas as pl
from jax.experimental.pallas import tpu as pltpu
from jax.sharding import PartitionSpec as P

BLOCK = 128
HALO = 128
PAD = 2 * HALO
MESH = pl.DeviceIdType.MESH
F32 = jnp.float32
BF16 = jnp.bfloat16


def one_hot(matches):
    return jnp.where(matches, 1.0, 0.0).astype(BF16)


def groups_of(count):
    return 9 if count % 9 == 0 else 1


def slab_kernel(
    region, length, scale, parts,
    feat, gout, w1, w2, rule, rule_t, live,
    grad_in, total_out,
    fext, aext, gpad, hpad, rpad, wc, hots, spread, spread2, picks, hidden, gext, rims, rim_in,
    send, recv, partial, send_there, recv_there, send_back, recv_back, *held
):
    rows, chans = feat.shape
    offsets = w1.shape[0]
    blocks = rows // BLOCK
    ext_blocks = blocks + 2
    window = 3 * BLOCK
    group = groups_of(offsets)
    me = lax.axis_index("block")
    left, right = me - 1, me + 1
    has_left, has_right = me > 0, me < length - 1

    def copies(i, low, low_there, high, high_there):
        down = pltpu.make_async_remote_copy(
            src_ref=low, dst_ref=low_there, send_sem=send.at[i, 0], recv_sem=recv.at[i, 0],
            device_id={"block": left}, device_id_type=MESH)
        up = pltpu.make_async_remote_copy(
            src_ref=high, dst_ref=high_there, send_sem=send.at[i, 1], recv_sem=recv.at[i, 1],
            device_id={"block": right}, device_id_type=MESH)
        return down, up

    def start(pair):
        down, up = pair
        pl.when(has_left)(down.start)
        pl.when(has_right)(up.start)

    def finish(pair):
        down, up = pair

        @pl.when(has_left)
        def _():
            down.wait_send()
            up.wait_recv()

        @pl.when(has_right)
        def _():
            up.wait_send()
            down.wait_recv()

    stages, peers = sum_stages(
        region, length, scale, parts, partial, total_out, held,
        send_there, recv_there, send_back, recv_back)
    barrier = pltpu.get_barrier_semaphore()
    for peer in peers:
        pl.semaphore_signal(barrier, inc=1, device_id=peer, device_id_type=MESH)

    @pl.when(has_left)
    def _():
        pl.semaphore_signal(barrier, inc=1, device_id={"block": left}, device_id_type=MESH)

    @pl.when(has_right)
    def _():
        pl.semaphore_signal(barrier, inc=1, device_id={"block": right}, device_id_type=MESH)

    pl.semaphore_wait(
        barrier, len(peers) + has_left.astype(jnp.int32) + has_right.astype(jnp.int32))

    lower, upper = pl.ds(0, HALO), pl.ds(HALO + rows, HALO)
    own_low, own_high = pl.ds(HALO, HALO), pl.ds(rows, HALO)
    feat_copies = copies(0, feat.at[pl.ds(0, HALO)], fext.at[upper],
                         feat.at[pl.ds(rows - HALO, HALO)], fext.at[lower])
    act_copies = copies(1, aext.at[own_low], aext.at[upper], aext.at[own_high], aext.at[lower])
    rim_copies = [
        copies(2 + i, rims.at[i, 0], rim_in.at[i, 0], rims.at[i, 1], rim_in.at[i, 1])
        for i in range(2)
    ]
    start(feat_copies)

    edge = jnp.zeros((HALO, chans), BF16)

    @pl.when(jnp.logical_not(has_left))
    def _():
        fext[lower] = edge
        aext[lower] = edge
        for i in range(2):
            rim_in[i, 1] = edge

    @pl.when(jnp.logical_not(has_right))
    def _():
        fext[upper] = edge
        aext[upper] = edge
        for i in range(2):
            rim_in[i, 0] = edge

    fext[pl.ds(HALO, rows)] = feat[...]
    border = jnp.zeros((PAD, chans), BF16)
    for padded in (gpad, hpad):
        padded[pl.ds(0, PAD)] = border
        padded[pl.ds(PAD + rows, PAD)] = border
    gpad[pl.ds(PAD, rows)] = gout[...]
    nowhere = jnp.full((offsets, PAD), -1, jnp.int32)
    rpad[:, pl.ds(0, PAD)] = nowhere
    rpad[:, pl.ds(PAD + rows, PAD)] = nowhere
    rpad[:, pl.ds(PAD, rows)] = rule[...]

    def beside(weights):
        for k in range(offsets):
            wc[:, k * chans:(k + 1) * chans] = weights[k]

    def spread_rows(e, first, group, out, source):
        begin = pl.multiple_of(e * BLOCK, BLOCK)
        got = jnp.dot(hots[e, first * BLOCK:(first + group) * BLOCK, :],
                      source[pl.ds(begin, window)], preferred_element_type=F32).astype(BF16)
        for j in range(group):
            out[pl.ds(begin, BLOCK), (first + j) * chans:(first + j + 1) * chans] = (
                got[j * BLOCK:(j + 1) * BLOCK])

    def through_weights(source, i):
        @pl.loop(0, ext_blocks)
        def _(e):
            begin = pl.multiple_of(e * BLOCK, BLOCK)
            gext[pl.ds(begin, BLOCK)] = lax.dot_general(
                source[pl.ds(begin, BLOCK)], wc[...], (((1,), (1,)), ((), ())),
                preferred_element_type=F32)
        rims[i, 0] = gext[lower].astype(BF16)
        rims[i, 1] = gext[upper].astype(BF16)
        start(rim_copies[i])

    def take_rims(i):
        finish(rim_copies[i])
        gext[own_low] = gext[own_low] + rim_in[i, 1].astype(F32)
        gext[own_high] = gext[own_high] + rim_in[i, 0].astype(F32)

    def kernel_grad(extended, source, i):
        turned = extended[...].T
        first, last, base, size = parts[i]
        count = last - first
        unit = next(u for u in (4, 3, 2, 1) if count % u == 0)

        @pl.loop(0, count // unit)
        def _(g):
            begin = pl.multiple_of((first + g * unit) * chans, chans)
            got = jnp.dot(turned, source[:, pl.ds(begin, unit * chans)],
                          preferred_element_type=F32)
            for j in range(unit):
                at = pl.multiple_of(base + (g * unit + j) * chans, chans)
                partial[pl.ds(at, chans)] = got[:, j * chans:(j + 1) * chans]
        tail = size - count * chans
        if tail:
            partial[pl.ds(base + count * chans, tail)] = jnp.zeros((tail, chans), F32)

    @pl.loop(0, ext_blocks)
    def _(e):
        begin = pl.multiple_of(e * BLOCK, BLOCK)
        target = lax.broadcasted_iota(jnp.int32, (BLOCK, window), 0) + e * BLOCK
        for first in range(0, offsets, group):
            for k in range(first, first + group):
                hots[e, k * BLOCK:(k + 1) * BLOCK, :] = one_hot(
                    rpad[k:k + 1, pl.ds(begin, window)] == target)
            spread_rows(e, first, group, spread, gpad)

    beside(w2)
    through_weights(spread, 0)

    finish(feat_copies)

    @pl.loop(0, blocks)
    def _(b):
        begin = pl.multiple_of(b * BLOCK, BLOCK)
        local = rule_t[pl.ds(begin, BLOCK)] - b * BLOCK
        columns = lax.broadcasted_iota(jnp.int32, (BLOCK, window), 1)
        framed = fext[pl.ds(begin, window)]
        for first in range(0, offsets, group):
            chosen = jnp.concatenate(
                [one_hot(local[:, k:k + 1] == columns) for k in range(first, first + group)], 0)
            got = jnp.dot(chosen, framed, preferred_element_type=F32).astype(BF16)
            for j in range(group):
                picks[:, (first + j) * chans:(first + j + 1) * chans] = (
                    got[j * BLOCK:(j + 1) * BLOCK])
        total = jnp.dot(picks[...], w1[...].reshape(offsets * chans, chans),
                        preferred_element_type=F32)
        hidden[pl.ds(begin, BLOCK)] = total
        aext[pl.ds(begin + HALO, BLOCK)] = (total / (1.0 + jnp.exp(-total))).astype(BF16)

    start(act_copies)
    take_rims(0)

    @pl.loop(0, blocks)
    def _(b):
        begin = pl.multiple_of(b * BLOCK, BLOCK)
        value = hidden[pl.ds(begin, BLOCK)]
        sigma = 1.0 / (1.0 + jnp.exp(-value))
        slope = sigma * (1.0 + value * (1.0 - sigma))
        hpad[pl.ds(begin + PAD, BLOCK)] = (gext[pl.ds(begin + HALO, BLOCK)] * slope).astype(BF16)

    finish(act_copies)
    kernel_grad(aext, spread, 2)
    ready, middle, later = stages(2), stages(0), stages(1)
    next(ready)
    cut = parts[0][1]
    portion = 8 if cut % 8 == 0 else cut

    @pl.loop(0, ext_blocks)
    def _(e):
        for first in range(0, cut, portion):
            spread_rows(e, first, portion, spread2, hpad)

    next(ready)
    kernel_grad(fext, spread2, 0)
    next(middle)

    @pl.loop(0, ext_blocks)
    def _(e):
        spread_rows(e, cut, offsets - cut, spread2, hpad)

    next(ready)
    next(middle)
    kernel_grad(fext, spread2, 1)
    next(later)
    beside(w1)
    through_weights(spread2, 1)
    next(ready)
    next(middle)
    next(later)
    take_rims(1)
    for b in range(blocks):
        at = pl.ds(b * BLOCK, BLOCK)
        keep = live[b].astype(F32)
        grad_in[at] = (keep * (gout[at].astype(F32) + gext[pl.ds(b * BLOCK + HALO, BLOCK)])
                       ).astype(BF16)
    for _ in range(5):
        next(ready, None)
        next(middle, None)
        next(later, None)


def slab_step(features, grad_out, w1, w2, rulebook, live_blocks, parts, scale):
    region, block = lax.axis_size("region"), lax.axis_size("block")
    planes, depth = region // 2 * 2, block // 2
    count = planes + depth - 1
    total = sum(part[3] for part in parts)

    def held_of(size):
        half = size // 2
        quarter = half // planes
        return [
            pltpu.VMEM((quarter, chans), F32),
            pltpu.VMEM((half, chans), BF16),
            pltpu.VMEM((quarter, chans), BF16),
            pltpu.VMEM((half, chans), F32),
            pltpu.VMEM((planes - 1, quarter, chans), BF16),
            pltpu.VMEM((depth - 1, quarter // depth, chans), BF16),
        ]

    rows, chans = features.shape
    offsets = w1.shape[0]
    ext = rows + 2 * HALO
    blocks = rows // BLOCK
    wide = offsets * chans
    vmem = pl.BlockSpec(memory_space=pltpu.VMEM)
    return pl.pallas_call(
        functools.partial(slab_kernel, region, block, scale, parts),
        out_shape=(
            jax.ShapeDtypeStruct((rows, chans), BF16),
            jax.ShapeDtypeStruct((total, chans), BF16),
        ),
        in_specs=[vmem] * 6 + [pl.BlockSpec(memory_space=pltpu.SMEM)],
        out_specs=(vmem, vmem),
        scratch_shapes=[
            pltpu.VMEM((ext, chans), BF16),
            pltpu.VMEM((ext, chans), BF16),
            pltpu.VMEM((rows + 2 * PAD, chans), BF16),
            pltpu.VMEM((rows + 2 * PAD, chans), BF16),
            pltpu.VMEM((offsets, rows + 2 * PAD), jnp.int32),
            pltpu.VMEM((chans, wide), BF16),
            pltpu.VMEM((blocks + 2, offsets * BLOCK, 3 * BLOCK), BF16),
            pltpu.VMEM((ext, wide), BF16),
            pltpu.VMEM((ext, wide), BF16),
            pltpu.VMEM((BLOCK, wide), BF16),
            pltpu.VMEM((rows, chans), F32),
            pltpu.VMEM((ext, chans), F32),
            pltpu.VMEM((2, 2, HALO, chans), BF16),
            pltpu.VMEM((2, 2, HALO, chans), BF16),
            pltpu.SemaphoreType.DMA((4, 2)),
            pltpu.SemaphoreType.DMA((4, 2)),
            pltpu.VMEM((total, chans), F32),
        ] + [pltpu.SemaphoreType.DMA((len(parts), count))] * 4 + [
            one for part in parts for one in held_of(part[3])],
        compiler_params=pltpu.CompilerParams(
            collective_id=0, has_side_effects=True, vmem_limit_bytes=64000000),
    )(features, grad_out, w1, w2, rulebook, rulebook.T, live_blocks)


def sum_stages(region, block, scale, parts, partial, total_out, held,
               send_there, recv_there, send_back, recv_back):
    planes, depth = region // 2 * 2, block // 2
    r, b = lax.axis_index("region"), lax.axis_index("block")
    c, y, x, z = lax.rem(r, 2), r // 2, lax.rem(b, 2), b // 2
    p = y * 2 + x

    def device(core, plane, deep):
        return {"region": plane // 2 * 2 + core, "block": deep * 2 + lax.rem(plane, 2)}

    partner = device(1 - c, p, z)
    plane_peers = [device(c, lax.rem(p + d, planes), z) for d in range(1, planes)]
    deep_peers = [device(c, p, lax.rem(z + d, depth)) for d in range(1, depth)]

    def at(index, size):
        return pl.ds(pl.multiple_of(index * size, 16), size)

    def remote(src, dst, sems, i, n, peer):
        copy = pltpu.make_async_remote_copy(
            src_ref=src, dst_ref=dst, send_sem=sems[0].at[i, n], recv_sem=sems[1].at[i, n],
            device_id=peer, device_id_type=MESH)
        copy.start()
        return copy

    there = (send_there, recv_there)
    back = (send_back, recv_back)

    def stages(i):
        base, size = parts[i][2:]
        part, out = partial.at[pl.ds(base, size)], total_out.at[pl.ds(base, size)]
        own, mine, rest, got1, got2, got3 = held[6 * i:6 * i + 6]
        half = size // 2
        quarter = half // planes
        piece = quarter // depth
        first = remote(part.at[at(1 - c, half)], got1, there, i, 0, partner)
        yield
        first.wait()
        mine[...] = (part[at(c, half)] + got1[...]).astype(BF16)
        second = [remote(mine.at[at(lax.rem(p + d, planes), quarter)], got2.at[d - 1],
                         there, i, d, plane_peers[d - 1]) for d in range(1, planes)]
        yield
        value = part[at(c * planes + p, quarter)] + got1[at(p, quarter)]
        for d in range(1, planes):
            second[d - 1].wait()
            value = value + got2[d - 1].astype(F32)
        own[...] = value
        rest[...] = value.astype(BF16)
        third = [remote(rest.at[at(lax.rem(z + d, depth), piece)], got3.at[d - 1],
                        there, i, planes - 1 + d, deep_peers[d - 1]) for d in range(1, depth)]
        yield
        value = own[at(z, piece)]
        for d in range(1, depth):
            third[d - 1].wait()
            value = value + got3[d - 1].astype(F32)
        place = at((c * planes + p) * depth + z, piece)
        out[place] = (value / scale).astype(BF16)
        for where, peers, base in (
            (place, deep_peers, planes),
            (at(c * planes + p, quarter), plane_peers, 1),
            (at(c, half), [partner], 0),
        ):
            moved = [remote(out.at[where], out.at[where], back, i, base + n, peer)
                     for n, peer in enumerate(peers)]
            yield
            for copy in moved:
                copy.wait()
        yield

    return stages, [partner] + plane_peers + deep_peers


def on_device(features, grad_out, w1, w2, rulebook, live_blocks):
    offsets, chans = w1.shape[0], w1.shape[1]
    devices = lax.axis_size("region") * lax.axis_size("block")
    step = 16 * devices
    cut = offsets * 3 // 5
    parts, base = [], 0
    for first, last in ((0, cut), (cut, offsets), (0, offsets)):
        size = ((last - first) * chans + step - 1) // step * step
        parts.append((first, last, base, size))
        base += size
    scale = float(features.shape[0] * devices) ** 0.5
    grad_in, both = slab_step(
        features, grad_out, w1, w2, rulebook, live_blocks, tuple(parts), scale)
    low, high, second = [
        both[base:base + (last - first) * chans].astype(F32) for first, last, base, _ in parts]
    first = jnp.concatenate([low, high], 0)
    return (grad_in, first.reshape(w1.shape), second.reshape(w1.shape))


def solution(mesh):
    return jax.shard_map(
        on_device,
        mesh=mesh,
        in_specs=(
            P(("region", "block"), None),
            P(("region", "block"), None),
            P(),
            P(),
            P(None, ("region", "block")),
            P(("region", "block")),
        ),
        out_specs=(P(("region", "block"), None), P(), P()),
        check_vma=False,
    )
```

```python
import functools

import jax
import jax.numpy as jnp
from jax import lax
from jax.experimental import pallas as pl
from jax.experimental.pallas import tpu as pltpu
from jax.sharding import PartitionSpec as P

BLOCK = 128
HALO = 128
PAD = 2 * HALO
MESH = pl.DeviceIdType.MESH
F32 = jnp.float32
BF16 = jnp.bfloat16


def one_hot(matches):
    return jnp.where(matches, 1.0, 0.0).astype(BF16)


def groups_of(count):
    return 9 if count % 9 == 0 else 1


def slab_kernel(
    region, length, scale,
    feat, gout, w1, w2, rule, rule_t, live,
    grad_in, total_out,
    fext, aext, gpad, hpad, rpad, wc, hots, spread, spread2, picks, hidden, gext, rims, rim_in,
    send, recv, partial, own, mine, rest, got1, got2, got3,
    send_there, recv_there, send_back, recv_back,
):
    rows, chans = feat.shape
    offsets = w1.shape[0]
    blocks = rows // BLOCK
    ext_blocks = blocks + 2
    window = 3 * BLOCK
    group = groups_of(offsets)
    part_rows = partial.shape[1]
    me = lax.axis_index("block")
    left, right = me - 1, me + 1
    has_left, has_right = me > 0, me < length - 1

    def copies(i, low, low_there, high, high_there):
        down = pltpu.make_async_remote_copy(
            src_ref=low, dst_ref=low_there, send_sem=send.at[i, 0], recv_sem=recv.at[i, 0],
            device_id={"block": left}, device_id_type=MESH)
        up = pltpu.make_async_remote_copy(
            src_ref=high, dst_ref=high_there, send_sem=send.at[i, 1], recv_sem=recv.at[i, 1],
            device_id={"block": right}, device_id_type=MESH)
        return down, up

    def start(pair):
        down, up = pair
        pl.when(has_left)(down.start)
        pl.when(has_right)(up.start)

    def finish(pair):
        down, up = pair

        @pl.when(has_left)
        def _():
            down.wait_send()
            up.wait_recv()

        @pl.when(has_right)
        def _():
            up.wait_send()
            down.wait_recv()

    stages, peers = sum_stages(
        region, length, scale, partial, total_out, own, mine, rest, got1, got2, got3,
        send_there, recv_there, send_back, recv_back)
    barrier = pltpu.get_barrier_semaphore()
    for peer in peers:
        pl.semaphore_signal(barrier, inc=1, device_id=peer, device_id_type=MESH)

    @pl.when(has_left)
    def _():
        pl.semaphore_signal(barrier, inc=1, device_id={"block": left}, device_id_type=MESH)

    @pl.when(has_right)
    def _():
        pl.semaphore_signal(barrier, inc=1, device_id={"block": right}, device_id_type=MESH)

    pl.semaphore_wait(
        barrier, len(peers) + has_left.astype(jnp.int32) + has_right.astype(jnp.int32))

    lower, upper = pl.ds(0, HALO), pl.ds(HALO + rows, HALO)
    own_low, own_high = pl.ds(HALO, HALO), pl.ds(rows, HALO)
    feat_copies = copies(0, feat.at[pl.ds(0, HALO)], fext.at[upper],
                         feat.at[pl.ds(rows - HALO, HALO)], fext.at[lower])
    act_copies = copies(1, aext.at[own_low], aext.at[upper], aext.at[own_high], aext.at[lower])
    rim_copies = [
        copies(2 + i, rims.at[i, 0], rim_in.at[i, 0], rims.at[i, 1], rim_in.at[i, 1])
        for i in range(2)
    ]
    start(feat_copies)

    edge = jnp.zeros((HALO, chans), BF16)

    @pl.when(jnp.logical_not(has_left))
    def _():
        fext[lower] = edge
        aext[lower] = edge
        for i in range(2):
            rim_in[i, 1] = edge

    @pl.when(jnp.logical_not(has_right))
    def _():
        fext[upper] = edge
        aext[upper] = edge
        for i in range(2):
            rim_in[i, 0] = edge

    fext[pl.ds(HALO, rows)] = feat[...]
    border = jnp.zeros((PAD, chans), BF16)
    for padded in (gpad, hpad):
        padded[pl.ds(0, PAD)] = border
        padded[pl.ds(PAD + rows, PAD)] = border
    gpad[pl.ds(PAD, rows)] = gout[...]
    nowhere = jnp.full((offsets, PAD), -1, jnp.int32)
    rpad[:, pl.ds(0, PAD)] = nowhere
    rpad[:, pl.ds(PAD + rows, PAD)] = nowhere
    rpad[:, pl.ds(PAD, rows)] = rule[...]

    def beside(weights):
        for k in range(offsets):
            wc[:, k * chans:(k + 1) * chans] = weights[k]

    def spread_rows(e, first, out, source):
        begin = pl.multiple_of(e * BLOCK, BLOCK)
        got = jnp.dot(hots[e, first * BLOCK:(first + group) * BLOCK, :],
                      source[pl.ds(begin, window)], preferred_element_type=F32).astype(BF16)
        for j in range(group):
            out[pl.ds(begin, BLOCK), (first + j) * chans:(first + j + 1) * chans] = (
                got[j * BLOCK:(j + 1) * BLOCK])

    def through_weights(source, i):
        @pl.loop(0, ext_blocks)
        def _(e):
            begin = pl.multiple_of(e * BLOCK, BLOCK)
            gext[pl.ds(begin, BLOCK)] = lax.dot_general(
                source[pl.ds(begin, BLOCK)], wc[...], (((1,), (1,)), ((), ())),
                preferred_element_type=F32)
        rims[i, 0] = gext[lower].astype(BF16)
        rims[i, 1] = gext[upper].astype(BF16)
        start(rim_copies[i])

    def take_rims(i):
        finish(rim_copies[i])
        gext[own_low] = gext[own_low] + rim_in[i, 1].astype(F32)
        gext[own_high] = gext[own_high] + rim_in[i, 0].astype(F32)

    def kernel_grad(extended, source, i):
        turned = extended[...].T

        @pl.loop(0, offsets // 3)
        def _(g):
            begin = pl.multiple_of(g * 3 * chans, chans)
            got = jnp.dot(turned, source[:, pl.ds(begin, 3 * chans)], preferred_element_type=F32)
            for j in range(3):
                at = pl.multiple_of((g * 3 + j) * chans, chans)
                partial[i, pl.ds(at, chans)] = got[:, j * chans:(j + 1) * chans]
        tail = part_rows - offsets * chans
        if tail:
            partial[i, pl.ds(offsets * chans, tail)] = jnp.zeros((tail, chans), F32)

    @pl.loop(0, ext_blocks)
    def _(e):
        begin = pl.multiple_of(e * BLOCK, BLOCK)
        target = lax.broadcasted_iota(jnp.int32, (BLOCK, window), 0) + e * BLOCK
        for first in range(0, offsets, group):
            for k in range(first, first + group):
                hots[e, k * BLOCK:(k + 1) * BLOCK, :] = one_hot(
                    rpad[k:k + 1, pl.ds(begin, window)] == target)
            spread_rows(e, first, spread, gpad)

    beside(w2)
    through_weights(spread, 0)

    finish(feat_copies)

    @pl.loop(0, blocks)
    def _(b):
        begin = pl.multiple_of(b * BLOCK, BLOCK)
        local = rule_t[pl.ds(begin, BLOCK)] - b * BLOCK
        columns = lax.broadcasted_iota(jnp.int32, (BLOCK, window), 1)
        framed = fext[pl.ds(begin, window)]
        for first in range(0, offsets, group):
            chosen = jnp.concatenate(
                [one_hot(local[:, k:k + 1] == columns) for k in range(first, first + group)], 0)
            got = jnp.dot(chosen, framed, preferred_element_type=F32).astype(BF16)
            for j in range(group):
                picks[:, (first + j) * chans:(first + j + 1) * chans] = (
                    got[j * BLOCK:(j + 1) * BLOCK])
        total = jnp.dot(picks[...], w1[...].reshape(offsets * chans, chans),
                        preferred_element_type=F32)
        hidden[pl.ds(begin, BLOCK)] = total
        aext[pl.ds(begin + HALO, BLOCK)] = (total / (1.0 + jnp.exp(-total))).astype(BF16)

    start(act_copies)
    take_rims(0)

    @pl.loop(0, blocks)
    def _(b):
        begin = pl.multiple_of(b * BLOCK, BLOCK)
        value = hidden[pl.ds(begin, BLOCK)]
        sigma = 1.0 / (1.0 + jnp.exp(-value))
        slope = sigma * (1.0 + value * (1.0 - sigma))
        hpad[pl.ds(begin + PAD, BLOCK)] = (gext[pl.ds(begin + HALO, BLOCK)] * slope).astype(BF16)

    finish(act_copies)
    kernel_grad(aext, spread, 1)
    ready, later = stages(1), stages(0)
    next(ready)

    def spread_blocks(begin, end):
        @pl.loop(begin, end)
        def _(e):
            for first in range(0, offsets, group):
                spread_rows(e, first, spread2, hpad)

    spread_blocks(0, ext_blocks // 2)
    next(ready)
    spread_blocks(ext_blocks // 2, ext_blocks)
    kernel_grad(fext, spread2, 0)
    next(later)
    next(ready)
    beside(w1)
    through_weights(spread2, 1)
    next(later)
    next(ready)
    take_rims(1)
    for b in range(blocks):
        at = pl.ds(b * BLOCK, BLOCK)
        keep = live[b].astype(F32)
        grad_in[at] = (keep * (gout[at].astype(F32) + gext[pl.ds(b * BLOCK + HALO, BLOCK)])
                       ).astype(BF16)
    for _ in range(5):
        next(ready, None)
        next(later, None)


def slab_step(features, grad_out, w1, w2, rulebook, live_blocks, part_rows, scale):
    region, block = lax.axis_size("region"), lax.axis_size("block")
    planes, depth = region // 2 * 2, block // 2
    half = part_rows // 2
    quarter = half // planes
    piece = quarter // depth
    count = planes + depth - 1
    rows, chans = features.shape
    offsets = w1.shape[0]
    ext = rows + 2 * HALO
    blocks = rows // BLOCK
    wide = offsets * chans
    vmem = pl.BlockSpec(memory_space=pltpu.VMEM)
    return pl.pallas_call(
        functools.partial(slab_kernel, region, block, scale),
        out_shape=(
            jax.ShapeDtypeStruct((rows, chans), BF16),
            jax.ShapeDtypeStruct((2, part_rows, chans), BF16),
        ),
        in_specs=[vmem] * 6 + [pl.BlockSpec(memory_space=pltpu.SMEM)],
        out_specs=(vmem, vmem),
        scratch_shapes=[
            pltpu.VMEM((ext, chans), BF16),
            pltpu.VMEM((ext, chans), BF16),
            pltpu.VMEM((rows + 2 * PAD, chans), BF16),
            pltpu.VMEM((rows + 2 * PAD, chans), BF16),
            pltpu.VMEM((offsets, rows + 2 * PAD), jnp.int32),
            pltpu.VMEM((chans, wide), BF16),
            pltpu.VMEM((blocks + 2, offsets * BLOCK, 3 * BLOCK), BF16),
            pltpu.VMEM((ext, wide), BF16),
            pltpu.VMEM((ext, wide), BF16),
            pltpu.VMEM((BLOCK, wide), BF16),
            pltpu.VMEM((rows, chans), F32),
            pltpu.VMEM((ext, chans), F32),
            pltpu.VMEM((2, 2, HALO, chans), BF16),
            pltpu.VMEM((2, 2, HALO, chans), BF16),
            pltpu.SemaphoreType.DMA((4, 2)),
            pltpu.SemaphoreType.DMA((4, 2)),
            pltpu.VMEM((2, part_rows, chans), F32),
            pltpu.VMEM((2, quarter, chans), F32),
            pltpu.VMEM((2, half, chans), BF16),
            pltpu.VMEM((2, quarter, chans), BF16),
            pltpu.VMEM((2, half, chans), F32),
            pltpu.VMEM((2, planes - 1, quarter, chans), BF16),
            pltpu.VMEM((2, depth - 1, piece, chans), BF16),
        ] + [pltpu.SemaphoreType.DMA((2, count))] * 4,
        compiler_params=pltpu.CompilerParams(
            collective_id=0, has_side_effects=True, vmem_limit_bytes=64000000),
    )(features, grad_out, w1, w2, rulebook, rulebook.T, live_blocks)


def sum_stages(region, block, scale, part, out, own, mine, rest, got1, got2, got3,
               send_there, recv_there, send_back, recv_back):
    half = part.shape[1] // 2
    planes, depth = region // 2 * 2, block // 2
    quarter = half // planes
    piece = quarter // depth
    r, b = lax.axis_index("region"), lax.axis_index("block")
    c, y, x, z = lax.rem(r, 2), r // 2, lax.rem(b, 2), b // 2
    p = y * 2 + x

    def device(core, plane, deep):
        return {"region": plane // 2 * 2 + core, "block": deep * 2 + lax.rem(plane, 2)}

    partner = device(1 - c, p, z)
    plane_peers = [device(c, lax.rem(p + d, planes), z) for d in range(1, planes)]
    deep_peers = [device(c, p, lax.rem(z + d, depth)) for d in range(1, depth)]

    def at(index, size):
        return pl.ds(pl.multiple_of(index * size, 16), size)

    def remote(src, dst, sems, i, n, peer):
        copy = pltpu.make_async_remote_copy(
            src_ref=src, dst_ref=dst, send_sem=sems[0].at[i, n], recv_sem=sems[1].at[i, n],
            device_id=peer, device_id_type=MESH)
        copy.start()
        return copy

    there = (send_there, recv_there)
    back = (send_back, recv_back)

    def stages(i):
        first = remote(part.at[i, at(1 - c, half)], got1.at[i], there, i, 0, partner)
        yield
        first.wait()
        mine[i] = (part[i, at(c, half)] + got1[i]).astype(BF16)
        second = [remote(mine.at[i, at(lax.rem(p + d, planes), quarter)], got2.at[i, d - 1],
                         there, i, d, plane_peers[d - 1]) for d in range(1, planes)]
        yield
        value = part[i, at(c * planes + p, quarter)] + got1[i, at(p, quarter)]
        for d in range(1, planes):
            second[d - 1].wait()
            value = value + got2[i, d - 1].astype(F32)
        own[i] = value
        rest[i] = value.astype(BF16)
        third = [remote(rest.at[i, at(lax.rem(z + d, depth), piece)], got3.at[i, d - 1],
                        there, i, planes - 1 + d, deep_peers[d - 1]) for d in range(1, depth)]
        yield
        value = own[i, at(z, piece)]
        for d in range(1, depth):
            third[d - 1].wait()
            value = value + got3[i, d - 1].astype(F32)
        place = at((c * planes + p) * depth + z, piece)
        out[i, place] = (value / scale).astype(BF16)
        for where, peers, base in (
            (place, deep_peers, planes),
            (at(c * planes + p, quarter), plane_peers, 1),
            (at(c, half), [partner], 0),
        ):
            moved = [remote(out.at[i, where], out.at[i, where], back, i, base + n, peer)
                     for n, peer in enumerate(peers)]
            yield
            for copy in moved:
                copy.wait()
        yield

    return stages, [partner] + plane_peers + deep_peers


def on_device(features, grad_out, w1, w2, rulebook, live_blocks):
    offsets, chans = w1.shape[0], w1.shape[1]
    devices = lax.axis_size("region") * lax.axis_size("block")
    step = 16 * devices
    part_rows = (offsets * chans + step - 1) // step * step
    scale = float(features.shape[0] * devices) ** 0.5
    grad_in, both = slab_step(
        features, grad_out, w1, w2, rulebook, live_blocks, part_rows, scale)
    both = both[:, :offsets * chans].astype(F32)
    both = both.reshape(2, offsets, chans, chans)
    return (grad_in, both[0], both[1])


def solution(mesh):
    return jax.shard_map(
        on_device,
        mesh=mesh,
        in_specs=(
            P(("region", "block"), None),
            P(("region", "block"), None),
            P(),
            P(),
            P(None, ("region", "block")),
            P(("region", "block")),
        ),
        out_specs=(P(("region", "block"), None), P(), P()),
        check_vma=False,
    )
```
